32 devices in a mesh: row: 4 (over z), col: 4 (over x, core), layer: 2 (over y).
Axes of the slice: x: 2, y: 2, z: 4, core: 2. Of those that a mesh axis runs over, the one named last changes fastest.
Arguments:
- intersection: bfloat16 [2048, 2, 1024], P('row', 'layer', 'col'), may hold values from -6 to 6
- density: bfloat16 [2, 1024, 2, 1024], P('layer', 'row', None, 'col'), may hold values from -0.125 to 0.125
- hamiltonian: bfloat16 [2, 1024, 2, 1024], P('layer', 'row', None, 'col'), may hold values from -0.125 to 0.125
- intersection_pattern: int32 [16, 2, 8], P('row', 'layer', 'col'), may hold values 0 or 1
- density_pattern: int32 [2, 8, 2, 8], P('layer', 'row', None, 'col'), may hold values 0 or 1
- hamiltonian_pattern: int32 [2, 8, 2, 8], P('layer', 'row', None, 'col'), may hold values 0 or 1
- product_filter: int32 [16, 2, 8], P('row', 'layer', 'col'), may hold values 0 or 1
Outputs:
- gradient_term: bfloat16 [2048, 2, 1024], P('row', 'layer', 'col')
The draws below stay inside these ranges and needn't reach their ends.
All inputs are finite; a program needn't handle non-finite values. No bound on the sum of `intersection_pattern` or of `density_pattern` or of `hamiltonian_pattern` or of `product_filter` on one device may be relied on, other than what follows from the above.
Results may differ from the reference program's by a relative error of at most 0.005.
Values may be sent and summed in bfloat16 or wider, within the bound.
No kernel may reach another device: no remote copies, remote signals or barrier semaphores. Data moves between devices by JAX's collectives and lax.ppermute only.
A program may use at most 64 MiB of HBM per device.

```python
import jax
import jax.numpy as jnp

BLOCK = 128
ORDER = 2048
HALF = 1024
NBLK = 16
HBLK = 8
N_LAYER = 2


def with_ends(drawn, key, low, top_value):
    spot = [jax.random.randint(jax.random.fold_in(key, axis), (), 0, length) for axis, length in enumerate(drawn.shape)]
    main_axis = drawn.shape.index(max(drawn.shape))
    beside = spot[:main_axis] + [(spot[main_axis] + 1) % drawn.shape[main_axis]] + spot[main_axis + 1:]
    return drawn.at[tuple(spot)].set(low).at[tuple(beside)].set(top_value)


def levels(key, shape, pieces, low, largest):
    factor_of, own = 1.0, jax.random.fold_in(key, 6)
    for dim, parts in pieces:
        draws = jnp.exp(jax.random.uniform(jax.random.fold_in(own, dim), (parts,), jnp.float32, low / len(pieces), largest / len(pieces)))
        factor_of = factor_of * jnp.repeat(draws, shape[dim] // parts).reshape([-1 if axis == dim else 1 for axis in range(len(shape))])
    return factor_of


def noise(stream_key, dims, scale, limit, cuts=(), dtype=jnp.bfloat16):
    level = levels(stream_key, dims, cuts, -0.22, 0.18) if cuts else 1.0
    values = jax.random.normal(stream_key, dims, jnp.float32) * scale * level
    return jnp.minimum(jnp.maximum(values, -limit), limit).astype(dtype)


def setup_inputs(seed: int = 0) -> dict:
    splits = jax.random.split(jax.random.key(seed), 8)
    return {
        "intersection": noise(splits[0], (ORDER, N_LAYER, HALF), 1.0, 6.0, ((0, 4), (1, 2), (2, 4))),
        "density": noise(splits[1], (N_LAYER, HALF, N_LAYER, HALF), ORDER ** -0.5, 0.125, ((0, 2), (1, 4), (3, 4))),
        "hamiltonian": noise(splits[2], (N_LAYER, HALF, N_LAYER, HALF), ORDER ** -0.5, 0.125, ((0, 2), (1, 4), (3, 4))),
        "intersection_pattern": with_ends((jax.random.randint(splits[3], (NBLK, N_LAYER, HBLK), 0, 4) < 3).astype(jnp.int32), jax.random.fold_in(splits[3], 1), 0, 1),
        "density_pattern": with_ends((jax.random.randint(splits[4], (N_LAYER, HBLK, N_LAYER, HBLK), 0, 4) < 3).astype(jnp.int32), jax.random.fold_in(splits[4], 1), 0, 1),
        "hamiltonian_pattern": with_ends((jax.random.randint(splits[5], (N_LAYER, HBLK, N_LAYER, HBLK), 0, 4) < 3).astype(jnp.int32), jax.random.fold_in(splits[5], 1), 0, 1),
        "product_filter": with_ends((jax.random.randint(splits[6], (NBLK, N_LAYER, HBLK), 0, 5) < 4).astype(jnp.int32), jax.random.fold_in(splits[6], 1), 0, 1),
    }


def widen(pattern):
    entries = jnp.repeat(pattern.astype(jnp.bfloat16), BLOCK, axis=0)
    return jnp.repeat(entries, BLOCK, axis=1)


def reference(intersection, density, hamiltonian, intersection_pattern, density_pattern, hamiltonian_pattern, product_filter):
    left_factor = intersection.reshape(ORDER, ORDER) * widen(intersection_pattern.reshape(NBLK, NBLK))
    right_factor = density.reshape(ORDER, ORDER) * widen(density_pattern.reshape(NBLK, NBLK))
    raw_product = jnp.dot(left_factor, right_factor, preferred_element_type=jnp.float32)
    filtered = raw_product.astype(jnp.bfloat16) * widen(product_filter.reshape(NBLK, NBLK))
    masked_ham = hamiltonian.reshape(ORDER, ORDER) * widen(hamiltonian_pattern.reshape(NBLK, NBLK))
    result = jnp.dot(filtered, masked_ham, preferred_element_type=jnp.float32)
    return result.astype(jnp.bfloat16).reshape(ORDER, N_LAYER, HALF)
```

```python
import jax
import jax.numpy as jnp
from jax import lax
from jax.experimental import pallas as pl
from jax.experimental.pallas import tpu as pltpu
from jax.sharding import PartitionSpec as P

BLOCK = 128
CORES = 2
VMEM_BYTES = 48 * 1024 * 1024


def masked(value, flag):
    return value * flag.astype(jnp.float32).astype(value.dtype)


def mask_kernel(s_ref, p_ref, h_ref, s_pat, p_pat, h_pat, s_out, p_own, p_other, h_own, h_other):
    layer = lax.axis_index("layer")
    for i in range(s_pat.shape[0]):
        for j in range(s_pat.shape[2]):
            at = (pl.ds(i * BLOCK, BLOCK), pl.ds(j * BLOCK, BLOCK))
            s_out[at] = masked(s_ref[at[0], 0, at[1]], s_pat[i, 0, j])
    for full, pat, own, other in ((p_ref, p_pat, p_own, p_other), (h_ref, h_pat, h_own, h_other)):
        for out, half in ((own, layer), (other, 1 - layer)):
            for i in range(pat.shape[1]):
                for j in range(pat.shape[3]):
                    at = (pl.ds(i * BLOCK, BLOCK), pl.ds(j * BLOCK, BLOCK))
                    out[at] = masked(full[half, at[0], at[1]], pat[0, i, half, j])


def mask_all(s, p, h, s_pat, p_pat, h_pat):
    rows, _, cols = s.shape
    k_rows = p.shape[1]
    tile = jax.ShapeDtypeStruct((k_rows, cols), s.dtype)
    vmem = pl.BlockSpec(memory_space=pltpu.VMEM)
    smem = pl.BlockSpec(memory_space=pltpu.SMEM)
    return pl.pallas_call(
        mask_kernel,
        out_shape=(jax.ShapeDtypeStruct((rows, cols), s.dtype), tile, tile, tile, tile),
        in_specs=[vmem] * 3 + [smem] * 3,
        out_specs=(vmem,) * 5,
        compiler_params=pltpu.CompilerParams(vmem_limit_bytes=VMEM_BYTES),
        name="mask_all",
    )(s, p[0].transpose(1, 0, 2), h[0].transpose(1, 0, 2), s_pat, p_pat, h_pat)


def product(left, right, pattern, half):
    rows, cols = left[0][1].shape
    k_rows = right[0][1].shape[0]
    n_left, n_right = len(left), len(right)

    def kernel(*refs):
        left_refs = refs[:n_left]
        right_refs = refs[n_left : n_left + n_right]
        rest = refs[n_left + n_right :]
        out, whole = rest[-2], rest[-1]
        row, col, layer = (lax.axis_index(a) for a in ("row", "col", "layer"))
        for (masks, _), ref in zip(right, right_refs):
            at = (layer ^ masks[1]) * half + (row ^ masks[0]) * k_rows
            whole[pl.ds(pl.multiple_of(at, k_rows), k_rows), :] = ref[...]
        total = jnp.zeros((rows, cols), jnp.float32)
        for (masks, _), ref in zip(left, left_refs):
            at = (layer ^ masks[1]) * half + (col ^ masks[0]) * cols
            total += jnp.dot(
                ref[...], whole[pl.ds(pl.multiple_of(at, cols), cols), :], preferred_element_type=jnp.float32
            )
        total = total.astype(jnp.bfloat16)
        if pattern is None:
            out[:, 0, :] = total
        else:
            out[...] = total
            for i in range(pattern.shape[0]):
                for j in range(pattern.shape[2]):
                    at = (pl.ds(i * BLOCK, BLOCK), pl.ds(j * BLOCK, BLOCK))
                    out[at] = masked(out[at], rest[0][i, 0, j])

    vmem = pl.BlockSpec(memory_space=pltpu.VMEM)
    smem = pl.BlockSpec(memory_space=pltpu.SMEM)
    extra = [] if pattern is None else [pattern]
    out_shape = (rows, 1, cols) if pattern is None else (rows, cols)
    return pl.pallas_call(
        kernel,
        out_shape=jax.ShapeDtypeStruct(out_shape, jnp.bfloat16),
        in_specs=[vmem] * (n_left + n_right) + [smem] * len(extra),
        out_specs=vmem,
        scratch_shapes=[pltpu.VMEM((2 * half, cols), jnp.bfloat16)],
        compiler_params=pltpu.CompilerParams(vmem_limit_bytes=VMEM_BYTES),
        name="product",
    )(*[t for _, t in left], *[t for _, t in right], *extra)


def exchange(value, axes, mask):
    sizes = [lax.axis_size(a) for a in axes]
    if len(axes) == 1:
        return lax.ppermute(value, axes[0], [(i, i ^ mask[0]) for i in range(sizes[0])])
    pairs = [
        (i * sizes[1] + j, (i ^ mask[0]) * sizes[1] + (j ^ mask[1])) for i in range(sizes[0]) for j in range(sizes[1])
    ]
    return lax.ppermute(value, axes, pairs)


def along_row(tile):
    have = [(0, tile)]
    mask = lax.axis_size("row") - 1
    while mask:
        have += [(m ^ mask, exchange(t, ("row",), (mask,))) for m, t in have]
        mask >>= 1
    return have


def over_plane(tile):
    have = [((0, 0), tile)]
    n_col = lax.axis_size("col")
    for m_col in range(0, n_col, CORES):
        for m_layer in range(2):
            if m_col or m_layer:
                have.append(((m_col, m_layer), exchange(tile, ("col", "layer"), (m_col, m_layer))))
    return have + [((m[0] ^ 1, m[1]), exchange(t, ("col",), (1,))) for m, t in have]


def gather_right(own, other):
    other = exchange(other, ("layer",), (1,))
    return [((m, 0), t) for m, t in along_row(own)] + [((m, 1), t) for m, t in along_row(other)]


def local(s, p, h, s_pat, p_pat, h_pat, keep):
    half = p.shape[1] * lax.axis_size("row")
    left, p_own, p_other, h_own, h_other = mask_all(s, p, h, s_pat, p_pat, h_pat)
    filtered = product(over_plane(left), gather_right(p_own, p_other), keep, half)
    return product(over_plane(filtered), gather_right(h_own, h_other), None, half)


def solution(mesh):
    left = P("row", "layer", "col")
    right = P("layer", "row", None, "col")
    return jax.shard_map(
        local,
        mesh=mesh,
        in_specs=(left, right, right, left, right, right, left),
        out_specs=left,
        check_vma=False,
    )
```

```python
import jax
import jax.numpy as jnp
from jax import lax
from jax.experimental import pallas as pl
from jax.experimental.pallas import tpu as pltpu
from jax.sharding import PartitionSpec as P

BLOCK = 128
CORES = 2
VMEM_BYTES = 48 * 1024 * 1024


def masked(value, flag):
    return value * flag.astype(jnp.float32).astype(value.dtype)


def blocks(rows, cols):
    return [
        (i, j, (pl.ds(i * BLOCK, BLOCK), pl.ds(j * BLOCK, BLOCK))) for i in range(rows) for j in range(cols)
    ]


def mask_kernel(s_ref, p_ref, h_ref, s_pat, p_pat, h_pat, s_out, p_own, h_own, others):
    layer = lax.axis_index("layer")
    k_rows, cols = p_own.shape
    for full, pat, own, first in ((p_ref, p_pat, p_own, 0), (h_ref, h_pat, h_own, k_rows)):
        for i, j, at in blocks(pat.shape[1], pat.shape[3]):
            own[at] = masked(full[layer, at[0], at[1]], pat[0, i, layer, j])
            there = (pl.ds(first + i * BLOCK, BLOCK), at[1])
            others[there] = masked(full[1 - layer, at[0], at[1]], pat[0, i, 1 - layer, j])
    for i, j, at in blocks(s_pat.shape[1], s_pat.shape[0]):
        s_out[at] = masked(s_ref[at], s_pat[j, i])


def flat_pattern(pattern):
    return pattern.transpose(1, 2, 0).reshape(pattern.shape[2], pattern.shape[0])


def mask_all(s, p, h, s_pat, p_pat, h_pat):
    rows, _, cols = s.shape
    k_rows = p.shape[1]
    shapes = ((rows, cols), (k_rows, cols), (k_rows, cols), (2 * k_rows, cols))
    smem = pl.BlockSpec(memory_space=pltpu.SMEM)

    def whole(shape):
        return pl.BlockSpec(shape, lambda i: (0,) * len(shape))

    return pl.pallas_call(
        mask_kernel,
        grid=(1,),
        out_shape=tuple(jax.ShapeDtypeStruct(shape, s.dtype) for shape in shapes),
        in_specs=[whole((rows, cols)), whole((2, k_rows, cols)), whole((2, k_rows, cols))] + [smem] * 3,
        out_specs=tuple(whole(shape) for shape in shapes),
        compiler_params=pltpu.CompilerParams(vmem_limit_bytes=VMEM_BYTES),
        name="mask_all",
    )(s.reshape(rows, cols), p[0].transpose(1, 0, 2), h[0].transpose(1, 0, 2), flat_pattern(s_pat), p_pat, h_pat)


def product(left, right, keep, half):
    rows, cols = left[0][1].shape
    n_left, n_right = len(left), len(right)

    def kernel(*refs):
        left_refs = refs[:n_left]
        right_refs = refs[n_left : n_left + n_right]
        rest = refs[n_left + n_right :]
        out, whole = rest[-2], rest[-1]
        row, col, layer = (lax.axis_index(a) for a in ("row", "col", "layer"))
        k_rows = half // lax.axis_size("row")
        for (mask, layers, _), ref in zip(right, right_refs):
            for n, m in enumerate(layers):
                at = (layer ^ m) * half + (row ^ mask) * k_rows
                whole[pl.ds(pl.multiple_of(at, k_rows), k_rows), :] = ref[pl.ds(n * k_rows, k_rows), :]
        total = jnp.zeros((rows, cols), jnp.float32)
        for (masks, _), ref in zip(left, left_refs):
            at = (layer ^ masks[1]) * half + (col ^ masks[0]) * cols
            total += jnp.dot(
                ref[...], whole[pl.ds(pl.multiple_of(at, cols), cols), :], preferred_element_type=jnp.float32
            )
        out[...] = total.astype(jnp.bfloat16)
        if keep is not None:
            for i, j, at in blocks(keep.shape[1], keep.shape[0]):
                out[at] = masked(out[at], rest[0][j, i])

    vmem = pl.BlockSpec(memory_space=pltpu.VMEM)
    extra = [] if keep is None else [keep]
    return pl.pallas_call(
        kernel,
        out_shape=jax.ShapeDtypeStruct((rows, cols), jnp.bfloat16),
        in_specs=[vmem] * (n_left + n_right) + [pl.BlockSpec(memory_space=pltpu.SMEM)] * len(extra),
        out_specs=vmem,
        scratch_shapes=[pltpu.VMEM((2 * half, cols), jnp.bfloat16)],
        compiler_params=pltpu.CompilerParams(vmem_limit_bytes=VMEM_BYTES),
        name="product",
    )(*[t for _, t in left], *[t for *_, t in right], *extra)


def exchange(value, axes, mask):
    sizes = [lax.axis_size(a) for a in axes]
    if len(axes) == 1:
        return lax.ppermute(value, axes[0], [(i, i ^ mask[0]) for i in range(sizes[0])])
    pairs = [
        (i * sizes[1] + j, (i ^ mask[0]) * sizes[1] + (j ^ mask[1])) for i in range(sizes[0]) for j in range(sizes[1])
    ]
    return lax.ppermute(value, axes, pairs)


def after(value, *others):
    return lax.optimization_barrier((value, *others))[0] if others else value


WAITS = {
    "s20": ("p1",),
    "sc00": ("ph",),
    "sc01": ("p2", "q2", "q1", "ph",),
    "sc20": ("p2", "q2", "ph",),
    "sc21": ("p2", "q2",),
    "q2": ("ph",),
    "s01": ("q1",),
}
ORDER = (
    "ph", "p3", "sc00", "p1", "q1", "s21", "q3", "s01", "s20", "p2", "q2", "h3", "h1", "sc01", "sc20",
    "sc21", "x", "x21", "x01", "x20", "h2", "xc00", "xc01", "xc20", "xc21",
)


class Exchanges:
    def __init__(self):
        self.done = {}

    def add(self, name, value, axes, mask):
        gates = [self.done[n] for n in WAITS.get(name, ()) if n in self.done]
        self.done[name] = exchange(after(value, *gates), axes, mask)


def row_steps():
    have, steps, distance = [0], [], lax.axis_size("row") - 1
    while distance:
        new = [(m ^ distance, m, distance) for m in have]
        steps += new
        have += [m for m, _, _ in new]
        distance >>= 1
    return steps


def local(s, p, h, s_pat, p_pat, h_pat, keep):
    k = p.shape[1]
    half = k * lax.axis_size("row")
    s0, p0, h0, ph0 = mask_all(s, p, h, s_pat, p_pat, h_pat)
    ex = Exchanges()
    done = ex.done
    plane = [(c, l) for c in range(0, lax.axis_size("col"), CORES) for l in range(2)][1:]
    whole = {}

    def h2():
        if not whole:
            whole[0] = jnp.concatenate([h0, done["ph"][k:]], axis=0)
        return whole[0]

    def step(kind, mask, source, distance):
        if kind == "p":
            return lambda: ex.add(f"p{mask}", done[f"p{source}"] if source else p0, ("row",), (distance,))
        if kind == "h":
            return lambda: ex.add(f"h{mask}", done[f"h{source}"] if source else h2(), ("row",), (distance,))
        if source:
            return lambda: ex.add(f"q{mask}", done[f"q{source}"], ("row",), (distance,))
        return lambda: ex.add(f"q{mask}", ph0[:k], ("row", "layer"), (distance, 1))

    def tiles(kind, own):
        return {(0, 0): own, **{m: done[f"{kind}{m[0]}{m[1]}"] for m in plane}}

    def between(kind, own, m):
        return lambda: ex.add(f"{kind}{m[0]}{m[1]}", own(), ("col", "layer"), m)

    def cores(kind, own, m):
        return lambda: ex.add(f"{kind}c{m[0]}{m[1]}", tiles(kind, own())[m] if m != (0, 0) else own(), ("col",), (1,))

    sends = {"ph": lambda: ex.add("ph", ph0, ("layer",), (1,))}
    for mask, source, distance in row_steps():
        for kind in "pqh":
            sends[f"{kind}{mask}"] = step(kind, mask, source, distance)
    def factor(kind, own):
        mine = tiles(kind, own)
        return list(mine.items()) + [((m[0] ^ 1, m[1]), done[f"{kind}c{m[0]}{m[1]}"]) for m in mine]

    masks = [mask for mask, _, _ in row_steps()]

    def first():
        right = [(0, (0,), p0), (0, (1,), done["ph"])]
        right += [(m, (n,), done[f"{kind}{m}"]) for n, kind in enumerate("pq") for m in masks]
        gates = [done[n] for n in WAITS.get("x", ()) if n in done]
        done["x"] = product(factor("s", after(s0, *gates)), right, flat_pattern(keep), half)

    for kind, own in (("s", lambda: s0), ("x", lambda: done["x"])):
        if kind == "x":
            sends["x"] = first
        for m in plane:
            sends[f"{kind}{m[0]}{m[1]}"] = between(kind, own, m)
        for m in [(0, 0)] + plane:
            sends[f"{kind}c{m[0]}{m[1]}"] = cores(kind, own, m)
    for name in ORDER if set(ORDER) == set(sends) else list(sends):
        sends[name]()
    right = [(0, (0, 1), h2())] + [(m, (0, 1), done[f"h{m}"]) for m in masks]
    return product(factor("x", done["x"]), right, None, half).reshape(s.shape)


def solution(mesh):
    left = P("row", "layer", "col")
    right = P("layer", "row", None, "col")
    return jax.shard_map(
        local,
        mesh=mesh,
        in_specs=(left, right, right, left, right, right, left),
        out_specs=left,
        check_vma=False,
    )
```

```python
import jax
import jax.numpy as jnp
from jax import lax
from jax.experimental import pallas as pl
from jax.experimental.pallas import tpu as pltpu
from jax.sharding import PartitionSpec as P

BLOCK = 128
CORES = 2
VMEM_BYTES = 48 * 1024 * 1024


def masked(value, flag):
    return value * flag.astype(jnp.float32).astype(value.dtype)


def blocks(rows, cols):
    return [
        (i, j, (pl.ds(i * BLOCK, BLOCK), pl.ds(j * BLOCK, BLOCK))) for i in range(rows) for j in range(cols)
    ]


def mask_kernel(s_ref, p_ref, h_ref, s_pat, p_pat, h_pat, s_out, p_own, h_own, others):
    layer = lax.axis_index("layer")
    k_rows, cols = p_own.shape
    for full, pat, own, first in ((p_ref, p_pat, p_own, 0), (h_ref, h_pat, h_own, k_rows)):
        for i, j, at in blocks(pat.shape[1], pat.shape[3]):
            own[at] = masked(full[layer, at[0], at[1]], pat[0, i, layer, j])
            there = (pl.ds(first + i * BLOCK, BLOCK), at[1])
            others[there] = masked(full[1 - layer, at[0], at[1]], pat[0, i, 1 - layer, j])
    for i, j, at in blocks(s_pat.shape[1], s_pat.shape[0]):
        s_out[at] = masked(s_ref[at], s_pat[j, i])


def flat_pattern(pattern):
    return pattern.transpose(1, 2, 0).reshape(pattern.shape[2], pattern.shape[0])


def mask_all(s, p, h, s_pat, p_pat, h_pat):
    rows, _, cols = s.shape
    k_rows = p.shape[1]
    shapes = ((rows, cols), (k_rows, cols), (k_rows, cols), (2 * k_rows, cols))
    smem = pl.BlockSpec(memory_space=pltpu.SMEM)

    def whole(shape):
        return pl.BlockSpec(shape, lambda i: (0,) * len(shape))

    return pl.pallas_call(
        mask_kernel,
        grid=(1,),
        out_shape=tuple(jax.ShapeDtypeStruct(shape, s.dtype) for shape in shapes),
        in_specs=[whole((rows, cols)), whole((2, k_rows, cols)), whole((2, k_rows, cols))] + [smem] * 3,
        out_specs=tuple(whole(shape) for shape in shapes),
        compiler_params=pltpu.CompilerParams(vmem_limit_bytes=VMEM_BYTES),
        name="mask_all",
    )(s.reshape(rows, cols), p[0].transpose(1, 0, 2), h[0].transpose(1, 0, 2), flat_pattern(s_pat), p_pat, h_pat)


def product(left, right, keep, half):
    rows, cols = left[0][1].shape
    n_left, n_right = len(left), len(right)

    def kernel(*refs):
        left_refs = refs[:n_left]
        right_refs = refs[n_left : n_left + n_right]
        rest = refs[n_left + n_right :]
        out, whole = rest[-2], rest[-1]
        row, col, layer = (lax.axis_index(a) for a in ("row", "col", "layer"))
        k_rows = half // lax.axis_size("row")
        for (mask, layers, _), ref in zip(right, right_refs):
            for n, m in enumerate(layers):
                at = (layer ^ m) * half + (row ^ mask) * k_rows
                whole[pl.ds(pl.multiple_of(at, k_rows), k_rows), :] = ref[pl.ds(n * k_rows, k_rows), :]
        total = jnp.zeros((rows, cols), jnp.float32)
        for (masks, _), ref in zip(left, left_refs):
            at = (layer ^ masks[1]) * half + (col ^ masks[0]) * cols
            total += jnp.dot(
                ref[...], whole[pl.ds(pl.multiple_of(at, cols), cols), :], preferred_element_type=jnp.float32
            )
        out[...] = total.astype(jnp.bfloat16)
        if keep is not None:
            for i, j, at in blocks(keep.shape[1], keep.shape[0]):
                out[at] = masked(out[at], rest[0][j, i])

    vmem = pl.BlockSpec(memory_space=pltpu.VMEM)
    extra = [] if keep is None else [keep]
    return pl.pallas_call(
        kernel,
        out_shape=jax.ShapeDtypeStruct((rows, cols), jnp.bfloat16),
        in_specs=[vmem] * (n_left + n_right) + [pl.BlockSpec(memory_space=pltpu.SMEM)] * len(extra),
        out_specs=vmem,
        scratch_shapes=[pltpu.VMEM((2 * half, cols), jnp.bfloat16)],
        compiler_params=pltpu.CompilerParams(vmem_limit_bytes=VMEM_BYTES),
        name="product",
    )(*[t for _, t in left], *[t for *_, t in right], *extra)


def exchange(value, axes, mask):
    sizes = [lax.axis_size(a) for a in axes]
    if len(axes) == 1:
        return lax.ppermute(value, axes[0], [(i, i ^ mask[0]) for i in range(sizes[0])])
    pairs = [
        (i * sizes[1] + j, (i ^ mask[0]) * sizes[1] + (j ^ mask[1])) for i in range(sizes[0]) for j in range(sizes[1])
    ]
    return lax.ppermute(value, axes, pairs)


def after(value, *others):
    return lax.optimization_barrier((value, *others))[0] if others else value


WAITS = {
    "s20": ("p1", "s01",),
    "sc00": ("p3",),
    "sc01": ("p2", "ph", "q1", "q2",),
    "sc20": ("p2", "ph", "q2", "s20",),
    "sc21": ("p2", "q2",),
    "q2": ("s01",),
    "ph": ("p3",),
}
ORDER = (
    "s01", "p3", "ph", "p1", "q1", "q3", "s20", "s21", "sc00", "p2", "q2", "h3", "h1", "sc01", "sc20",
    "sc21", "x", "x21", "x01", "x20", "h2", "xc00", "xc01", "xc20", "xc21",
)


class Exchanges:
    def __init__(self):
        self.done = {}

    def add(self, name, value, axes, mask):
        gates = [self.done[n] for n in WAITS.get(name, ()) if n in self.done]
        self.done[name] = exchange(after(value, *gates), axes, mask)


def row_steps():
    have, steps, distance = [0], [], lax.axis_size("row") - 1
    while distance:
        new = [(m ^ distance, m, distance) for m in have]
        steps += new
        have += [m for m, _, _ in new]
        distance >>= 1
    return steps


def local(s, p, h, s_pat, p_pat, h_pat, keep):
    k = p.shape[1]
    half = k * lax.axis_size("row")
    s0, p0, h0, ph0 = mask_all(s, p, h, s_pat, p_pat, h_pat)
    ex = Exchanges()
    done = ex.done
    plane = [(c, l) for c in range(0, lax.axis_size("col"), CORES) for l in range(2)][1:]
    whole = {}

    def h2():
        if not whole:
            whole[0] = jnp.concatenate([h0, done["ph"][k:]], axis=0)
        return whole[0]

    def step(kind, mask, source, distance):
        if kind == "p":
            return lambda: ex.add(f"p{mask}", done[f"p{source}"] if source else p0, ("row",), (distance,))
        if kind == "h":
            return lambda: ex.add(f"h{mask}", done[f"h{source}"] if source else h2(), ("row",), (distance,))
        if source:
            return lambda: ex.add(f"q{mask}", done[f"q{source}"], ("row",), (distance,))
        return lambda: ex.add(f"q{mask}", ph0[:k], ("row", "layer"), (distance, 1))

    def tiles(kind, own):
        return {(0, 0): own, **{m: done[f"{kind}{m[0]}{m[1]}"] for m in plane}}

    def between(kind, own, m):
        if kind == "s" and m[0] and m[1]:
            return lambda: ex.add(f"s{m[0]}{m[1]}", done["s01"], ("col",), (m[0],))
        return lambda: ex.add(f"{kind}{m[0]}{m[1]}", own(), ("col", "layer"), m)

    def cores(kind, own, m):
        return lambda: ex.add(f"{kind}c{m[0]}{m[1]}", tiles(kind, own())[m] if m != (0, 0) else own(), ("col",), (1,))

    sends = {"ph": lambda: ex.add("ph", ph0, ("layer",), (1,))}
    for mask, source, distance in row_steps():
        for kind in "pqh":
            sends[f"{kind}{mask}"] = step(kind, mask, source, distance)
    def factor(kind, own):
        mine = tiles(kind, own)
        return list(mine.items()) + [((m[0] ^ 1, m[1]), done[f"{kind}c{m[0]}{m[1]}"]) for m in mine]

    masks = [mask for mask, _, _ in row_steps()]

    def first():
        right = [(0, (0,), p0), (0, (1,), done["ph"])]
        right += [(m, (n,), done[f"{kind}{m}"]) for n, kind in enumerate("pq") for m in masks]
        gates = [done[n] for n in WAITS.get("x", ()) if n in done]
        done["x"] = product(factor("s", after(s0, *gates)), right, flat_pattern(keep), half)

    for kind, own in (("s", lambda: s0), ("x", lambda: done["x"])):
        if kind == "x":
            sends["x"] = first
        for m in plane:
            sends[f"{kind}{m[0]}{m[1]}"] = between(kind, own, m)
        for m in [(0, 0)] + plane:
            sends[f"{kind}c{m[0]}{m[1]}"] = cores(kind, own, m)
    for name in ORDER if set(ORDER) == set(sends) else list(sends):
        sends[name]()
    right = [(0, (0, 1), h2())] + [(m, (0, 1), done[f"h{m}"]) for m in masks]
    return product(factor("x", done["x"]), right, None, half).reshape(s.shape)


def solution(mesh):
    left = P("row", "layer", "col")
    right = P("layer", "row", None, "col")
    return jax.shard_map(
        local,
        mesh=mesh,
        in_specs=(left, right, right, left, right, right, left),
        out_specs=left,
        check_vma=False,
    )
```

```python
import jax
import jax.numpy as jnp
from jax import lax
from jax.experimental import pallas as pl
from jax.experimental.pallas import tpu as pltpu
from jax.sharding import PartitionSpec as P

BLOCK = 128
CORES = 2
VMEM_BYTES = 48 * 1024 * 1024


def masked(value, flag):
    return value * flag.astype(jnp.float32).astype(value.dtype)


def blocks(rows, cols):
    return [
        (i, j, (pl.ds(i * BLOCK, BLOCK), pl.ds(j * BLOCK, BLOCK))) for i in range(rows) for j in range(cols)
    ]


def mask_kernel(s_ref, p_ref, h_ref, s_pat, p_pat, h_pat, s_out, p_own, h_own, others):
    layer = lax.axis_index("layer")
    k_rows, cols = p_own.shape
    for full, pat, own, first in ((p_ref, p_pat, p_own, 0), (h_ref, h_pat, h_own, k_rows)):
        for i, j, at in blocks(pat.shape[1], pat.shape[3]):
            own[at] = masked(full[layer, at[0], at[1]], pat[0, i, layer, j])
            there = (pl.ds(first + i * BLOCK, BLOCK), at[1])
            others[there] = masked(full[1 - layer, at[0], at[1]], pat[0, i, 1 - layer, j])
    for i, j, at in blocks(s_pat.shape[1], s_pat.shape[0]):
        s_out[at] = masked(s_ref[at], s_pat[j, i])


def flat_pattern(pattern):
    return pattern.transpose(1, 2, 0).reshape(pattern.shape[2], pattern.shape[0])


def mask_all(s, p, h, s_pat, p_pat, h_pat):
    rows, _, cols = s.shape
    k_rows = p.shape[1]
    shapes = ((rows, cols), (k_rows, cols), (k_rows, cols), (2 * k_rows, cols))
    smem = pl.BlockSpec(memory_space=pltpu.SMEM)

    def whole(shape):
        return pl.BlockSpec(shape, lambda i: (0,) * len(shape))

    return pl.pallas_call(
        mask_kernel,
        grid=(1,),
        out_shape=tuple(jax.ShapeDtypeStruct(shape, s.dtype) for shape in shapes),
        in_specs=[whole((rows, cols)), whole((2, k_rows, cols)), whole((2, k_rows, cols))] + [smem] * 3,
        out_specs=tuple(whole(shape) for shape in shapes),
        compiler_params=pltpu.CompilerParams(vmem_limit_bytes=VMEM_BYTES),
        name="mask_all",
    )(s.reshape(rows, cols), p[0].transpose(1, 0, 2), h[0].transpose(1, 0, 2), flat_pattern(s_pat), p_pat, h_pat)


def product(left, right, keep, half):
    rows, cols = left[0][1].shape
    n_left, n_right = len(left), len(right)

    def kernel(*refs):
        left_refs = refs[:n_left]
        right_refs = refs[n_left : n_left + n_right]
        rest = refs[n_left + n_right :]
        out, whole = rest[-2], rest[-1]
        row, col, layer = (lax.axis_index(a) for a in ("row", "col", "layer"))
        k_rows = half // lax.axis_size("row")
        for (mask, layers, _), ref in zip(right, right_refs):
            for n, m in enumerate(layers):
                at = (layer ^ m) * half + (row ^ mask) * k_rows
                whole[pl.ds(pl.multiple_of(at, k_rows), k_rows), :] = ref[pl.ds(n * k_rows, k_rows), :]
        at = [(layer ^ m[1]) * half + (col ^ m[0]) * cols for m, _ in left]
        right_tiles = [whole[pl.ds(pl.multiple_of(x, cols), cols), :] for x in at]
        out[...] = jnp.dot(
            jnp.concatenate([ref[...] for ref in left_refs], axis=1),
            jnp.concatenate(right_tiles, axis=0),
            preferred_element_type=jnp.float32,
        ).astype(jnp.bfloat16)
        if keep is not None:
            for i, j, at in blocks(keep.shape[1], keep.shape[0]):
                out[at] = masked(out[at], rest[0][j, i])

    vmem = pl.BlockSpec(memory_space=pltpu.VMEM)
    extra = [] if keep is None else [keep]
    return pl.pallas_call(
        kernel,
        out_shape=jax.ShapeDtypeStruct((rows, cols), jnp.bfloat16),
        in_specs=[vmem] * (n_left + n_right) + [pl.BlockSpec(memory_space=pltpu.SMEM)] * len(extra),
        out_specs=vmem,
        scratch_shapes=[pltpu.VMEM((2 * half, cols), jnp.bfloat16)],
        compiler_params=pltpu.CompilerParams(vmem_limit_bytes=VMEM_BYTES),
        name="product",
    )(*[t for _, t in left], *[t for *_, t in right], *extra)


def exchange(value, axes, mask):
    sizes = [lax.axis_size(a) for a in axes]
    if len(axes) == 1:
        return lax.ppermute(value, axes[0], [(i, i ^ mask[0]) for i in range(sizes[0])])
    pairs = [
        (i * sizes[1] + j, (i ^ mask[0]) * sizes[1] + (j ^ mask[1])) for i in range(sizes[0]) for j in range(sizes[1])
    ]
    return lax.ppermute(value, axes, pairs)


def after(value, *others):
    return lax.optimization_barrier((value, *others))[0] if others else value


WAITS = {
    "s20": ("p1", "s01",),
    "sc00": ("p3",),
    "sc01": ("p2", "ph", "q1", "q2",),
    "sc20": ("p2", "ph", "q2", "s20",),
    "sc21": ("p2", "q2",),
    "q2": ("s01",),
    "ph": ("p3",),
}
ORDER = (
    "s01", "p3", "ph", "p1", "q1", "q3", "s20", "s21", "sc00", "p2", "q2", "h3", "h1", "sc01", "sc20",
    "sc21", "x", "x21", "x01", "x20", "h2", "xc00", "xc01", "xc20", "xc21",
)


class Exchanges:
    def __init__(self):
        self.done = {}

    def add(self, name, value, axes, mask):
        gates = [self.done[n] for n in WAITS.get(name, ()) if n in self.done]
        self.done[name] = exchange(after(value, *gates), axes, mask)


def row_steps():
    have, steps, distance = [0], [], lax.axis_size("row") - 1
    while distance:
        new = [(m ^ distance, m, distance) for m in have]
        steps += new
        have += [m for m, _, _ in new]
        distance >>= 1
    return steps


def local(s, p, h, s_pat, p_pat, h_pat, keep):
    k = p.shape[1]
    half = k * lax.axis_size("row")
    s0, p0, h0, ph0 = mask_all(s, p, h, s_pat, p_pat, h_pat)
    ex = Exchanges()
    done = ex.done
    plane = [(c, l) for c in range(0, lax.axis_size("col"), CORES) for l in range(2)][1:]
    whole = {}

    def h2():
        if not whole:
            whole[0] = jnp.concatenate([h0, done["ph"][k:]], axis=0)
        return whole[0]

    def step(kind, mask, source, distance):
        if kind == "p":
            return lambda: ex.add(f"p{mask}", done[f"p{source}"] if source else p0, ("row",), (distance,))
        if kind == "h":
            return lambda: ex.add(f"h{mask}", done[f"h{source}"] if source else h2(), ("row",), (distance,))
        if source:
            return lambda: ex.add(f"q{mask}", done[f"q{source}"], ("row",), (distance,))
        return lambda: ex.add(f"q{mask}", ph0[:k], ("row", "layer"), (distance, 1))

    def tiles(kind, own):
        return {(0, 0): own, **{m: done[f"{kind}{m[0]}{m[1]}"] for m in plane}}

    def between(kind, own, m):
        if kind == "s" and m[0] and m[1]:
            return lambda: ex.add(f"s{m[0]}{m[1]}", done["s01"], ("col",), (m[0],))
        return lambda: ex.add(f"{kind}{m[0]}{m[1]}", own(), ("col", "layer"), m)

    def cores(kind, own, m):
        return lambda: ex.add(f"{kind}c{m[0]}{m[1]}", tiles(kind, own())[m] if m != (0, 0) else own(), ("col",), (1,))

    sends = {"ph": lambda: ex.add("ph", ph0, ("layer",), (1,))}
    for mask, source, distance in row_steps():
        for kind in "pqh":
            sends[f"{kind}{mask}"] = step(kind, mask, source, distance)
    def factor(kind, own):
        mine = tiles(kind, own)
        return list(mine.items()) + [((m[0] ^ 1, m[1]), done[f"{kind}c{m[0]}{m[1]}"]) for m in mine]

    masks = [mask for mask, _, _ in row_steps()]

    def first():
        right = [(0, (0,), p0), (0, (1,), done["ph"])]
        right += [(m, (n,), done[f"{kind}{m}"]) for n, kind in enumerate("pq") for m in masks]
        gates = [done[n] for n in WAITS.get("x", ()) if n in done]
        done["x"] = product(factor("s", after(s0, *gates)), right, flat_pattern(keep), half)

    for kind, own in (("s", lambda: s0), ("x", lambda: done["x"])):
        if kind == "x":
            sends["x"] = first
        for m in plane:
            sends[f"{kind}{m[0]}{m[1]}"] = between(kind, own, m)
        for m in [(0, 0)] + plane:
            sends[f"{kind}c{m[0]}{m[1]}"] = cores(kind, own, m)
    for name in ORDER if set(ORDER) == set(sends) else list(sends):
        sends[name]()
    right = [(0, (0, 1), h2())] + [(m, (0, 1), done[f"h{m}"]) for m in masks]
    return product(factor("x", done["x"]), right, None, half).reshape(s.shape)


def solution(mesh):
    left = P("row", "layer", "col")
    right = P("layer", "row", None, "col")
    return jax.shard_map(
        local,
        mesh=mesh,
        in_specs=(left, right, right, left, right, right, left),
        out_specs=left,
        check_vma=False,
    )
```
